256 devices in a mesh: row: 64 (over z, y, core), col: 4 (over x).
Axes of the slice: x: 4, y: 4, z: 8, core: 2. Of those that a mesh axis runs over, the one named last changes fastest.
Arguments:
- train_points: float32 [16, 3, 64, 128], P(None, None, 'row'), may hold values from -6 to 6
- new_points: float32 [16, 256], replicated, may hold values from -6 to 6
- lengthscales: float32 [16], replicated, may hold values from 2.5 to 6
- factor: float32 [3, 64, 128, 3, 4, 2048], P(None, 'row', None, None, 'col'), may hold values from -0.02734375 to 0.02734375
- diag_inverse: float32 [3, 64, 128, 4, 2048], P(None, 'row', None, 'col'), may hold values from -3 to 3
Outputs:
- solution: float32 [3, 4, 64, 32, 256], P(None, 'col', 'row')
The draws below stay inside these ranges and needn't reach their ends.
All inputs are finite; a program needn't handle non-finite values.
Results may differ from the reference program's by a relative error of at most 0.0001.
Values sent between devices are 32-bit elements; how exact they have to be, the bound alone decides.
No kernel may reach another device: no remote copies, remote signals or barrier semaphores. Data moves between devices by JAX's collectives and lax.ppermute only.
A program may use at most 128 MiB of HBM per device.

```python
import math
import jax
import jax.numpy as jnp
from jax import lax

DIMS = 16
NEW = 256
PANELS = 3
RB = 128
PW = 8192
QW = 2048
QR = 32
TRAIN = 24576
N_ROW = 64
N_COL = 4


def draw_diag_inverse(key, part):
    first_key, second_key = jax.random.split(jax.random.fold_in(key, 7))
    shape = (PANELS, PW // RB, RB, PW // QW, QW)
    in_index = lax.broadcasted_iota(jnp.int32, shape, 1) * RB + lax.broadcasted_iota(jnp.int32, shape, 2)
    out_index = lax.broadcasted_iota(jnp.int32, shape, 3) * QW + lax.broadcasted_iota(jnp.int32, shape, 4)
    below = jnp.clip(jax.random.normal(first_key, shape, jnp.float32), -3.0, 3.0)
    middle = jax.random.uniform(second_key, shape, jnp.float32, 0.6, 1.6)
    below = below * (0.7 / math.sqrt(PW))
    values = jnp.where(out_index == in_index, middle, jnp.where(out_index > in_index, below, 0.0))
    return values.astype(jnp.float32)


def block_scale(rng, extent, shards, low, high):
    gain = 1.0
    for axis_at, blocks in shards:
        draws = jax.random.uniform(jax.random.fold_in(jax.random.fold_in(rng, 6), axis_at), (blocks,), jnp.float32, low / len(shards), high / len(shards))
        gain = gain * jnp.repeat(jnp.exp(draws), extent[axis_at] // blocks).reshape((-1,) + (1,) * (len(extent) - 1 - axis_at))
    return gain


def scatter_about(stream_key, shape, scale, most, cuts=(), held_as=jnp.bfloat16):
    result = jax.random.normal(stream_key, shape, jnp.float32) * scale
    if len(cuts) > 0:
        result = block_scale(stream_key, shape, cuts, -0.22, 0.18) * result
    return jnp.clip(result, min=-most, max=most).astype(held_as)


def setup_inputs(seed: int = 0) -> dict:
    key_of = jax.random.split(jax.random.key(seed), 6)
    return {
        "train_points": scatter_about(key_of[0], (DIMS, PANELS, N_ROW, RB), 1.0, 6.0, ((2, 64),), jnp.float32),
        "new_points": scatter_about(key_of[1], (DIMS, NEW), 1.0, 6.0, (), jnp.float32),
        "lengthscales": jnp.clip(jnp.exp(jax.random.uniform(key_of[2], (DIMS,), jnp.float32, math.log(2.5), math.log(6.0))), 2.5, 6.0),
        "factor": scatter_about(key_of[3], (PANELS, N_ROW, RB, PANELS, N_COL, QW), (2 * TRAIN) ** -0.5, 0.02734375, ((1, 64), (4, 4)), jnp.float32),
        "diag_inverse": draw_diag_inverse(jax.random.fold_in(key_of[5], 71), 0),
    }


def reference(train_points, new_points, lengthscales, factor, diag_inverse):
    highest = lax.Precision.HIGHEST
    scaled_train = (train_points / lengthscales[:, None, None, None]).reshape(DIMS, TRAIN)
    scaled_new = new_points / lengthscales[:, None]
    inner_products = jnp.dot(scaled_train.T, scaled_new, precision=highest)
    sqdist = (jnp.sum(scaled_train * scaled_train, axis=0)[:, None]
              + jnp.sum(scaled_new * scaled_new, axis=0)[None, :] - 2.0 * inner_products)
    kernel = jnp.exp(-0.5 * sqdist)
    matrix = factor.reshape(TRAIN, TRAIN)
    inverses = diag_inverse.reshape(PANELS, PW, PW)
    pieces = []
    for panel in range(PANELS):
        first_row = panel * PW
        residual = kernel[first_row:first_row + PW]
        if panel > 0:
            solved_rows = jnp.concatenate(pieces, axis=0)
            residual = residual - jnp.dot(matrix[first_row:first_row + PW, :first_row], solved_rows, precision=highest)
        pieces.append(jnp.dot(inverses[panel].T, residual, precision=highest))
    solution = jnp.concatenate(pieces, axis=0)
    return solution.reshape(PANELS, N_COL, N_ROW, QR, NEW)
```

```python
import jax
import jax.numpy as jnp
from jax import lax
from jax.sharding import Mesh, PartitionSpec as P

Z, Y, CORE = 8, 4, 2
HIGH = lax.Precision.HIGH


def shift(value, axis, by, size):
    return lax.ppermute(value, axis, [(i, (i + by) % size) for i in range(size)])


def pick(value, at, axis):
    return lax.dynamic_index_in_dim(value, at, axis=axis, keepdims=False)


def scatter_sum(product):
    core, y = lax.axis_index("core"), lax.axis_index("y")
    new = product.shape[1]
    parts = product.reshape(Z, Y, CORE, -1, new)
    other = shift(pick(parts, 1 - core, 2), "core", 1, CORE)
    chip = pick(parts, core, 2) + other
    chunks = [pick(chip, (y + by) % Y, 1) for by in range(Y)]
    arrived = [shift(chunks[by], "y", by, Y) for by in (2, 1, 3)]
    line = chunks[0] + arrived[0] + arrived[1] + arrived[2]
    line = lax.all_to_all(line, "z", 0, 0)
    return jnp.sum(line, axis=0)


def gather(rows):
    core, y = lax.axis_index("core"), lax.axis_index("y")
    line = lax.all_to_all(jnp.broadcast_to(rows[None], (Z,) + rows.shape), "z", 0, 0)
    by_y = [line] + [shift(line, "y", by, Y) for by in (1, 2, 3)]
    mine = jnp.stack(by_y)
    other = jnp.stack([shift(piece, "core", 1, CORE) for piece in by_y])
    by_core = jnp.stack([mine, other])
    by_core = jnp.where(core == 0, by_core, by_core[::-1])
    by_core = jnp.stack([pick(by_core, (y - at) % Y, 1) for at in range(Y)], axis=1)
    return by_core.transpose(2, 1, 0, 3, 4).reshape(-1, rows.shape[1])


def on_device(train_points, new_points, lengthscales, factor, diag_inverse):
    panels = factor.shape[0]
    block_rows = factor.shape[2]
    quarter_cols = factor.shape[5]
    new_count = new_points.shape[1]
    scaled_train = (train_points / lengthscales[:, None, None, None]).reshape(
        train_points.shape[0], panels * block_rows
    )
    scaled_new = new_points / lengthscales[:, None]
    inner_products = jnp.dot(scaled_train.T, scaled_new, precision=lax.Precision.HIGHEST)
    sqdist = (
        jnp.sum(scaled_train * scaled_train, axis=0)[:, None]
        + jnp.sum(scaled_new * scaled_new, axis=0)[None, :]
        - 2.0 * inner_products
    )
    kernel = jnp.exp(-0.5 * sqdist).reshape(panels, block_rows, new_count)
    factor_blocks = factor.reshape(panels, block_rows, panels, quarter_cols)
    inverse_blocks = diag_inverse.reshape(panels, block_rows, quarter_cols)

    solved = []
    partial = [None] * panels
    for panel in range(panels):
        residual = kernel[panel]
        if panel > 0:
            own = partial[panel]
            others = [shift(own, "col", by, 4) for by in (2, 1, 3)]
            residual = residual - (own + others[0] + others[1] + others[2])
        product = jnp.einsum("iq,im->qm", inverse_blocks[panel], residual, precision=HIGH)
        rows = scatter_sum(product)
        solved.append(rows)
        if panel + 1 < panels:
            quarter = gather(rows)
            for later in range(panel + 1, panels):
                change = jnp.dot(factor_blocks[later, :, panel], quarter, precision=HIGH)
                partial[later] = change if partial[later] is None else partial[later] + change
    return jnp.stack(solved)[:, None, None]


def solution(mesh):
    split = Mesh(
        mesh.devices.reshape(Z, Y, CORE, mesh.devices.shape[1]), ("z", "y", "core", "col")
    )
    row = ("z", "y", "core")
    return jax.shard_map(
        on_device,
        mesh=split,
        in_specs=(
            P(None, None, row, None),
            P(),
            P(),
            P(None, row, None, None, "col", None),
            P(None, row, None, "col", None),
        ),
        out_specs=P(None, "col", row, None, None),
        check_vma=False,
    )
```

```python
import functools

import jax
import jax.numpy as jnp
from jax import lax
from jax.experimental import pallas as pl
from jax.experimental.pallas import tpu as pltpu
from jax.sharding import Mesh, PartitionSpec as P

Z, Y, CORE, N_COL = 8, 4, 2, 4
LANES = 128


def shift(value, axis, by, size):
    return lax.ppermute(value, axis, [(i, (i + by) % size) for i in range(size)])


def halves(value):
    high = value.astype(jnp.bfloat16)
    return high, (value - high.astype(jnp.float32)).astype(jnp.bfloat16)


def dot3(left, right, contract):
    left_high, left_low = left
    right_high, right_low = right
    dot = functools.partial(
        lax.dot_general,
        dimension_numbers=(contract, ((), ())),
        preferred_element_type=jnp.float32,
    )
    return dot(left_low, right_high) + dot(left_high, right_low) + dot(left_high, right_high)


def split_kernel(n_blocks, place, *refs):
    block_refs, extra_refs, outs, flat = refs[:n_blocks], refs[n_blocks : -Y - 1], refs[-Y - 1 : -1], refs[-1]
    y = place[1]
    rows, columns = flat.shape
    half = columns // (Z * Y)
    for at, block_ref in enumerate(block_refs):
        flat[...] = block_ref[...].reshape(rows, columns)
        left = lax.broadcasted_iota(jnp.int32, (rows, LANES), 1) < half
        for e in range(Y):
            to = lax.rem(y + e, Y)
            odd = lax.rem(to, 2) == 1
            for pair in range(Z // 2):
                tiles = []
                for z in (2 * pair, 2 * pair + 1):
                    start = pl.multiple_of((z * 2 + to // 2) * LANES, LANES)
                    tiles.append(flat[:, pl.ds(start, LANES)])
                first, second = tiles
                value = jnp.where(
                    left,
                    jnp.where(odd, pltpu.roll(first, half, axis=1), first),
                    jnp.where(odd, second, pltpu.roll(second, half, axis=1)),
                )
                outs[e][at, :rows, pair * LANES : (pair + 1) * LANES] = value
    for points_ref in extra_refs:
        more = points_ref.shape[0] // 2
        points = points_ref[...].reshape(2 * more, LANES)
        for out_ref in outs:
            out_ref[0, rows:, :] = jnp.zeros((more, out_ref.shape[2]), jnp.float32)
            out_ref[0, rows:, :LANES] = points[:more]
            out_ref[0, rows:, LANES : 2 * LANES] = points[more:]


def split_columns(place, blocks, extra=None):
    specs, arrays = [], []
    rows, columns = blocks[0][0].shape[2], blocks[0][0].shape[-1]
    for array, at in blocks:
        arrays.append(array)
        if array.ndim == 5:
            specs.append(
                pl.BlockSpec((None, None, rows, None, columns), lambda i, place, at=at: (at[0], 0, 0, 0, 0))
            )
        else:
            specs.append(
                pl.BlockSpec(
                    (None, None, rows, None, None, columns),
                    lambda i, place, at=at: (at[0], 0, 0, at[1], 0, 0),
                )
            )
    more = 0
    if extra is not None:
        arrays.append(extra)
        dims, _, _, width = extra.shape
        specs.append(pl.BlockSpec((dims, None, None, width), lambda i, place: (0, 0, 0, 0)))
        more = dims // 2
    out = jax.ShapeDtypeStruct((len(blocks), rows + more, columns // Y), jnp.float32)
    return pl.pallas_call(
        functools.partial(split_kernel, len(blocks)),
        out_shape=[out] * Y,
        grid_spec=pltpu.PrefetchScalarGridSpec(
            num_scalar_prefetch=1,
            grid=(1,),
            in_specs=specs,
            out_specs=[pl.BlockSpec(out.shape, lambda i, place: (0, 0, 0))] * Y,
            scratch_shapes=[pltpu.VMEM((rows, columns), jnp.float32)],
        ),
        cost_estimate=pl.CostEstimate(
            flops=len(blocks) * rows * columns,
            bytes_accessed=len(blocks) * rows * columns * 8,
            transcendentals=0,
        ),
        compiler_params=pltpu.CompilerParams(vmem_limit_bytes=54 << 20),
    )(place, *arrays)


def inverse_kernel(place, *refs):
    residuals, blocks = refs[:Y], refs[Y : 2 * Y]
    keep_ref, send_ref, high, low, product = refs[2 * Y :]
    core = place[2]
    rows = blocks[0].shape[0]
    parts = [halves(ref[...]) for ref in residuals]
    residual = tuple(jnp.concatenate([part[i] for part in parts]) for i in range(2))
    for e in range(Y):
        high[e * rows : (e + 1) * rows, :], low[e * rows : (e + 1) * rows, :] = halves(blocks[e][...])
    columns = high.shape[1]
    step = 256
    for start in range(0, columns, step):
        part = slice(start, start + step)
        product[part, :] = dot3((high[:, part], low[:, part]), residual, ((0,), (0,)))
    share = keep_ref.shape[1]
    for z in range(Z):
        for out_ref, owner in ((send_ref, 1 - core), (keep_ref, core)):
            start = pl.multiple_of((z * CORE + owner) * share, share)
            out_ref[z] = product[pl.ds(start, share), :]


def apply_inverse(place, residuals, blocks):
    rows, new = residuals[0].shape
    columns = blocks[0].shape[-1]
    out = jax.ShapeDtypeStruct((Z, columns // (Z * CORE), new), jnp.float32)
    return pl.pallas_call(
        inverse_kernel,
        out_shape=(out, out),
        grid_spec=pltpu.PrefetchScalarGridSpec(
            num_scalar_prefetch=1,
            grid=(1,),
            in_specs=[pl.BlockSpec((rows, new), lambda i, place: (0, 0))] * Y
            + [pl.BlockSpec((None, rows, columns), lambda i, place: (0, 0, 0))] * Y,
            out_specs=[pl.BlockSpec(out.shape, lambda i, place: (0, 0, 0))] * 2,
            scratch_shapes=[pltpu.VMEM((Y * rows, columns), jnp.bfloat16)] * 2
            + [pltpu.VMEM((columns, new), jnp.float32)],
        ),
        cost_estimate=pl.CostEstimate(
            flops=6 * Y * rows * columns * new, bytes_accessed=4 << 20, transcendentals=0
        ),
        compiler_params=pltpu.CompilerParams(vmem_limit_bytes=32 << 20),
    )(place, *residuals, *blocks)


def halve_kernel(block_ref, high_ref, low_ref, flat):
    flat[...] = block_ref[...]
    step = 16

    def part(i, carry):
        where = pl.ds(pl.multiple_of(i * step, step), step)
        high_ref[where, :], low_ref[where, :] = halves(flat[where, :])
        return carry

    lax.fori_loop(0, flat.shape[0] // step, part, 0)


def halve_block(factor, row, column):
    rows, columns = factor.shape[2], factor.shape[5]
    out = jax.ShapeDtypeStruct((rows, columns), jnp.bfloat16)
    return pl.pallas_call(
        halve_kernel,
        out_shape=(out, out),
        grid=(1,),
        in_specs=[
            pl.BlockSpec(
                (None, None, rows, None, None, columns), lambda i: (row, 0, 0, column, 0, 0)
            )
        ],
        out_specs=[pl.BlockSpec(out.shape, lambda i: (0, 0))] * 2,
        scratch_shapes=[pltpu.VMEM(out.shape, jnp.float32)],
        cost_estimate=pl.CostEstimate(
            flops=4 * rows * columns, bytes_accessed=8 * rows * columns, transcendentals=0
        ),
        compiler_params=pltpu.CompilerParams(vmem_limit_bytes=56 << 20),
    )(factor)


def factor_kernel(place, block_high, block_low, *refs):
    pieces, rest, (out_ref, high, low) = refs[: Y + 1], refs[Y + 1], refs[Y + 2 :]
    y, core = place[1], place[2]
    share = pieces[0].shape[1]

    def put(z, carry):
        for at, owner in enumerate((core, 1 - core)):
            for e in range(Y):
                row = (z * Y + lax.rem(y + Y - e, Y)) * CORE + owner
                where = pl.ds(pl.multiple_of(row * share, share), share)
                piece = rest[e - 1, z] if at and e else pieces[at * Y + e][z]
                high[where, :], low[where, :] = halves(piece)
        return carry

    lax.fori_loop(0, Z, put, 0)
    out_ref[...] = dot3(
        (block_high[...], block_low[...]), (high[...], low[...]), ((1,), (0,))
    )


def apply_factor(place, block, pieces):
    rows, columns = block[0].shape
    new = pieces[0].shape[-1]
    return pl.pallas_call(
        factor_kernel,
        out_shape=jax.ShapeDtypeStruct((rows, new), jnp.float32),
        grid_spec=pltpu.PrefetchScalarGridSpec(
            num_scalar_prefetch=1,
            grid=(1,),
            in_specs=[pl.BlockSpec((rows, columns), lambda i, place: (0, 0))] * 2
            + [pl.BlockSpec(pieces[0].shape, lambda i, place: (0, 0, 0))] * (Y + 1)
            + [pl.BlockSpec(pieces[-1].shape, lambda i, place: (0, 0, 0, 0))],
            out_specs=pl.BlockSpec((rows, new), lambda i, place: (0, 0)),
            scratch_shapes=[pltpu.VMEM((columns, new), jnp.bfloat16)] * 2,
        ),
        cost_estimate=pl.CostEstimate(
            flops=6 * rows * columns * new, bytes_accessed=3 << 20, transcendentals=0
        ),
        compiler_params=pltpu.CompilerParams(vmem_limit_bytes=32 << 20),
    )(place, *block, *pieces)


def spread(arrays, steps=(2, 1, 3)):
    return {e: shift(arrays[e], "y", e, Y) for e in steps}


def in_order(own, arrived):
    return [own] + [arrived[e] for e in range(1, Y)]


def kernel_rows(scaled_train, scaled_new):
    inner_products = jnp.dot(scaled_train.T, scaled_new, precision=lax.Precision.HIGHEST)
    sqdist = (
        jnp.sum(scaled_train * scaled_train, axis=0)[:, None]
        + jnp.sum(scaled_new * scaled_new, axis=0)[None, :]
        - 2.0 * inner_products
    )
    return jnp.exp(-0.5 * sqdist)


def on_device(train_points, new_points, lengthscales, factor, diag_inverse):
    dims, panels, _, block_rows = train_points.shape
    new_count = new_points.shape[1]
    place = jnp.stack([lax.axis_index(axis) for axis in ("z", "y", "core")]).astype(jnp.int32)
    scaled_new = new_points / lengthscales[:, None]

    w0 = split_columns(place, [(diag_inverse, (0,))], train_points)
    w0 = in_order(w0[0], spread(w0))
    w1 = split_columns(place, [(diag_inverse, (1,))])
    w2 = split_columns(place, [(diag_inverse, (2,))])
    l10, l20, l21 = (halve_block(factor, *at) for at in ((1, 0), (2, 0), (2, 1)))
    w0, w1, l10, l20 = lax.optimization_barrier((w0, w1, l10, l20))

    own_points = (train_points[:, 1:, 0] / lengthscales[:, None, None]).reshape(dims, -1)
    kernel = kernel_rows(own_points, scaled_new).reshape(panels - 1, block_rows, new_count)

    both = jnp.concatenate([part[0, block_rows:, : 2 * block_rows] for part in w0]).reshape(
        Y, dims // 2, 2, block_rows
    )
    line_points = both.transpose(2, 1, 0, 3).reshape(dims, Y, block_rows)
    line_points = (line_points / lengthscales[:, None, None]).reshape(dims, -1)
    residuals = kernel_rows(line_points, scaled_new).reshape(Y, block_rows, new_count)
    residuals = [residuals[e] for e in range(Y)]

    def reduce(keep, send):
        chip = keep + shift(send, "core", 1, CORE)
        return jnp.sum(lax.all_to_all(chip, "z", 0, 0), axis=0)

    def gather_z(rows):
        return lax.all_to_all(jnp.broadcast_to(rows[None], (Z,) + rows.shape), "z", 0, 0)

    def gather(line):
        mine = in_order(line, spread({e: line for e in range(1, Y)}))
        rest = shift(jnp.stack(mine[1:]), "core", 1, CORE)
        return mine + [shift(line, "core", 1, CORE), rest]

    def residual_rows(panel, own):
        arrived = [shift(own, "col", by, N_COL) for by in (2, 1, 3)]
        rest = kernel[panel - 1] - (own + arrived[0] + arrived[1] + arrived[2])
        return in_order(rest, spread({e: rest for e in range(1, Y)}))

    def solve(residuals, blocks, later, during_sum, during_gather):
        rows = reduce(*apply_inverse(place, residuals, blocks))
        far = spread(later, (2,))
        rows, far, later, during_sum = lax.optimization_barrier((rows, far, later, during_sum))
        line = gather_z(rows)
        near = spread(later, (1, 3))
        line, near, during_gather = lax.optimization_barrier((line, near, during_gather))
        return rows, line, in_order(later[0], {**far, **near}), during_sum, during_gather

    rows_0, line, w1, w2, l21 = solve(residuals, w0, w1, w2, l21)
    pieces = gather(line)
    residuals = residual_rows(1, apply_factor(place, l10, pieces))
    early = apply_factor(place, l20, pieces)

    residuals, w2, early = lax.optimization_barrier((residuals, w2, early))
    rows_1, line, w2, _, _ = solve(residuals, w1, w2, (), ())
    pieces = gather(line)
    residuals = residual_rows(2, early + apply_factor(place, l21, pieces))

    rows_2 = reduce(*apply_inverse(place, residuals, w2))
    return jnp.stack([rows_0, rows_1, rows_2])[:, None, None]


def solution(mesh):
    split = Mesh(
        mesh.devices.reshape(Z, Y, CORE, mesh.devices.shape[1]), ("z", "y", "core", "col")
    )
    row = ("z", "y", "core")
    return jax.shard_map(
        on_device,
        mesh=split,
        in_specs=(
            P(None, None, row, None),
            P(),
            P(),
            P(None, row, None, None, "col", None),
            P(None, row, None, "col", None),
        ),
        out_specs=P(None, "col", row, None, None),
        check_vma=False,
    )
```

```python
import functools

import jax
import jax.numpy as jnp
from jax import lax
from jax.experimental import pallas as pl
from jax.experimental.pallas import tpu as pltpu
from jax.sharding import Mesh, PartitionSpec as P

Z, Y, CORE, N_COL = 8, 4, 2, 4
LANES = 128


def shift(value, axis, by, size):
    return lax.ppermute(value, axis, [(i, (i + by) % size) for i in range(size)])


def halves(value):
    high = value.astype(jnp.bfloat16)
    return high, (value - high.astype(jnp.float32)).astype(jnp.bfloat16)


def dot3(left, right, contract):
    left_high, left_low = left
    right_high, right_low = right
    dot = functools.partial(
        lax.dot_general,
        dimension_numbers=(contract, ((), ())),
        preferred_element_type=jnp.float32,
    )
    return dot(left_low, right_high) + dot(left_high, right_low) + dot(left_high, right_high)


def split_kernel(n_blocks, place, *refs):
    block_refs, extra_refs, outs, flat = refs[:n_blocks], refs[n_blocks : -Y - 1], refs[-Y - 1 : -1], refs[-1]
    y = place[1]
    rows, columns = flat.shape
    half = columns // (Z * Y)
    for at, block_ref in enumerate(block_refs):
        flat[...] = block_ref[...].reshape(rows, columns)
        left = lax.broadcasted_iota(jnp.int32, (rows, LANES), 1) < half
        for e in range(Y):
            to = lax.rem(y + e, Y)
            odd = lax.rem(to, 2) == 1
            for pair in range(Z // 2):
                tiles = []
                for z in (2 * pair, 2 * pair + 1):
                    start = pl.multiple_of((z * 2 + to // 2) * LANES, LANES)
                    tiles.append(flat[:, pl.ds(start, LANES)])
                first, second = tiles
                value = jnp.where(
                    left,
                    jnp.where(odd, pltpu.roll(first, half, axis=1), first),
                    jnp.where(odd, second, pltpu.roll(second, half, axis=1)),
                )
                outs[e][at, :rows, pair * LANES : (pair + 1) * LANES] = value
    for points_ref in extra_refs:
        more = points_ref.shape[0] // 2
        points = points_ref[...].reshape(2 * more, LANES)
        for out_ref in outs:
            out_ref[0, rows:, :] = jnp.zeros((more, out_ref.shape[2]), jnp.float32)
            out_ref[0, rows:, :LANES] = points[:more]
            out_ref[0, rows:, LANES : 2 * LANES] = points[more:]


def split_columns(place, blocks, extra=None):
    specs, arrays = [], []
    rows, columns = blocks[0][0].shape[2], blocks[0][0].shape[-1]
    for array, at in blocks:
        arrays.append(array)
        if array.ndim == 5:
            specs.append(
                pl.BlockSpec((None, None, rows, None, columns), lambda i, place, at=at: (at[0], 0, 0, 0, 0))
            )
        else:
            specs.append(
                pl.BlockSpec(
                    (None, None, rows, None, None, columns),
                    lambda i, place, at=at: (at[0], 0, 0, at[1], 0, 0),
                )
            )
    more = 0
    if extra is not None:
        arrays.append(extra)
        dims, _, _, width = extra.shape
        specs.append(pl.BlockSpec((dims, None, None, width), lambda i, place: (0, 0, 0, 0)))
        more = dims // 2
    out = jax.ShapeDtypeStruct((len(blocks), rows + more, columns // Y), jnp.float32)
    return pl.pallas_call(
        functools.partial(split_kernel, len(blocks)),
        out_shape=[out] * Y,
        grid_spec=pltpu.PrefetchScalarGridSpec(
            num_scalar_prefetch=1,
            grid=(1,),
            in_specs=specs,
            out_specs=[pl.BlockSpec(out.shape, lambda i, place: (0, 0, 0))] * Y,
            scratch_shapes=[pltpu.VMEM((rows, columns), jnp.float32)],
        ),
        cost_estimate=pl.CostEstimate(
            flops=len(blocks) * rows * columns,
            bytes_accessed=len(blocks) * rows * columns * 8,
            transcendentals=0,
        ),
        compiler_params=pltpu.CompilerParams(vmem_limit_bytes=54 << 20),
    )(place, *arrays)


def inverse_kernel(place, *refs):
    residuals, blocks = refs[:Y], refs[Y : 2 * Y]
    keep_ref, send_ref, high, low, product = refs[2 * Y :]
    core = place[2]
    rows = blocks[0].shape[0]
    parts = [halves(ref[...]) for ref in residuals]
    residual = tuple(jnp.concatenate([part[i] for part in parts]) for i in range(2))
    for e in range(Y):
        high[e * rows : (e + 1) * rows, :], low[e * rows : (e + 1) * rows, :] = halves(blocks[e][...])
    columns = high.shape[1]
    step = 256
    for start in range(0, columns, step):
        part = slice(start, start + step)
        product[part, :] = dot3((high[:, part], low[:, part]), residual, ((0,), (0,)))
    share = keep_ref.shape[1]
    for z in range(Z):
        for out_ref, owner in ((send_ref, 1 - core), (keep_ref, core)):
            start = pl.multiple_of((z * CORE + owner) * share, share)
            out_ref[z] = product[pl.ds(start, share), :]


def apply_inverse(place, residuals, blocks):
    rows, new = residuals[0].shape
    columns = blocks[0].shape[-1]
    out = jax.ShapeDtypeStruct((Z, columns // (Z * CORE), new), jnp.float32)
    return pl.pallas_call(
        inverse_kernel,
        out_shape=(out, out),
        grid_spec=pltpu.PrefetchScalarGridSpec(
            num_scalar_prefetch=1,
            grid=(1,),
            in_specs=[pl.BlockSpec((rows, new), lambda i, place: (0, 0))] * Y
            + [pl.BlockSpec((None, rows, columns), lambda i, place: (0, 0, 0))] * Y,
            out_specs=[pl.BlockSpec(out.shape, lambda i, place: (0, 0, 0))] * 2,
            scratch_shapes=[pltpu.VMEM((Y * rows, columns), jnp.bfloat16)] * 2
            + [pltpu.VMEM((columns, new), jnp.float32)],
        ),
        cost_estimate=pl.CostEstimate(
            flops=6 * Y * rows * columns * new, bytes_accessed=4 << 20, transcendentals=0
        ),
        compiler_params=pltpu.CompilerParams(vmem_limit_bytes=32 << 20),
    )(place, *residuals, *blocks)


def cores_kernel(n_blocks, place, *refs):
    block_refs, (own_ref, other_ref, flat) = refs[:n_blocks], refs[n_blocks:]
    core = place[2]
    rows, columns = flat.shape
    share = columns // (Z * Y * CORE)
    group = lax.broadcasted_iota(jnp.int32, (rows, LANES), 1) // share
    for at, block_ref in enumerate(block_refs):
        flat[...] = block_ref[...]
        for tile in range(columns // LANES // 2):
            first = flat[:, 2 * tile * LANES : (2 * tile + 1) * LANES]
            second = flat[:, (2 * tile + 1) * LANES : (2 * tile + 2) * LANES]

            def turned(value, groups):
                return pltpu.roll(value, groups % 4 * share, axis=1) if groups % 4 else value

            parts = [
                jnp.where(
                    group < 2,
                    jnp.where(group == 0, turned(first, -h), turned(first, -1 - h)),
                    jnp.where(group == 2, turned(second, 2 - h), turned(second, 1 - h)),
                )
                for h in range(CORE)
            ]
            where = slice(tile * LANES, (tile + 1) * LANES)
            own_ref[at, :, where] = jnp.where(core == 0, parts[0], parts[1])
            other_ref[at, :, where] = jnp.where(core == 0, parts[1], parts[0])


def split_cores(place, factor, blocks):
    rows, columns = factor.shape[2], factor.shape[5]
    out = jax.ShapeDtypeStruct((len(blocks), rows, columns // CORE), jnp.float32)
    return pl.pallas_call(
        functools.partial(cores_kernel, len(blocks)),
        out_shape=(out, out),
        grid_spec=pltpu.PrefetchScalarGridSpec(
            num_scalar_prefetch=1,
            grid=(1,),
            in_specs=[
                pl.BlockSpec(
                    (None, None, rows, None, None, columns),
                    lambda i, place, at=at: (at[0], 0, 0, at[1], 0, 0),
                )
                for at in blocks
            ],
            out_specs=[pl.BlockSpec(out.shape, lambda i, place: (0, 0, 0))] * 2,
            scratch_shapes=[pltpu.VMEM((rows, columns), jnp.float32)],
        ),
        cost_estimate=pl.CostEstimate(
            flops=8 * len(blocks) * rows * columns,
            bytes_accessed=8 * len(blocks) * rows * columns,
            transcendentals=0,
        ),
        compiler_params=pltpu.CompilerParams(vmem_limit_bytes=56 << 20),
    )(place, *[factor] * len(blocks))


def factor_kernel(place, own_ref, other_ref, *refs):
    pieces, (mine_ref, theirs_ref, high, low) = refs[:Y], refs[Y:]
    y = place[1]
    share = pieces[0].shape[1]

    def put(z, carry):
        for e in range(Y):
            row = z * Y + lax.rem(y + Y - e, Y)
            where = pl.ds(pl.multiple_of(row * share, share), share)
            high[where, :], low[where, :] = halves(pieces[e][z])
        return carry

    lax.fori_loop(0, Z, put, 0)
    for block_ref, out_ref in ((other_ref, theirs_ref), (own_ref, mine_ref)):
        out_ref[...] = dot3(halves(block_ref[...]), (high[...], low[...]), ((1,), (0,)))


def apply_factor(place, at, block, pieces):
    rows, columns = block[0].shape[1:]
    new = pieces[0].shape[-1]
    out = jax.ShapeDtypeStruct((rows, new), jnp.float32)
    return pl.pallas_call(
        factor_kernel,
        out_shape=(out, out),
        grid_spec=pltpu.PrefetchScalarGridSpec(
            num_scalar_prefetch=1,
            grid=(1,),
            in_specs=[pl.BlockSpec((None, rows, columns), lambda i, place: (at, 0, 0))] * 2
            + [pl.BlockSpec(pieces[0].shape, lambda i, place: (0, 0, 0))] * Y,
            out_specs=[pl.BlockSpec((rows, new), lambda i, place: (0, 0))] * 2,
            scratch_shapes=[pltpu.VMEM((columns, new), jnp.bfloat16)] * 2,
        ),
        cost_estimate=pl.CostEstimate(
            flops=12 * rows * columns * new, bytes_accessed=3 << 20, transcendentals=0
        ),
        compiler_params=pltpu.CompilerParams(vmem_limit_bytes=32 << 20),
    )(place, *block, *pieces)


def spread(arrays, steps=(2, 1, 3)):
    return {e: shift(arrays[e], "y", e, Y) for e in steps}


def in_order(own, arrived):
    return [own] + [arrived[e] for e in range(1, Y)]


def kernel_rows(scaled_train, scaled_new):
    inner_products = jnp.dot(scaled_train.T, scaled_new, precision=lax.Precision.HIGHEST)
    sqdist = (
        jnp.sum(scaled_train * scaled_train, axis=0)[:, None]
        + jnp.sum(scaled_new * scaled_new, axis=0)[None, :]
        - 2.0 * inner_products
    )
    return jnp.exp(-0.5 * sqdist)


def on_device(train_points, new_points, lengthscales, factor, diag_inverse):
    dims, panels, _, block_rows = train_points.shape
    new_count = new_points.shape[1]
    place = jnp.stack([lax.axis_index(axis) for axis in ("z", "y", "core")]).astype(jnp.int32)
    scaled_new = new_points / lengthscales[:, None]

    w0 = split_columns(place, [(diag_inverse, (0,))], train_points)
    w0 = in_order(w0[0], spread(w0))
    w1 = split_columns(place, [(diag_inverse, (1,))])
    w2 = split_columns(place, [(diag_inverse, (2,))])
    own_a, other_a = split_cores(place, factor, [(1, 0), (2, 0)])
    own_b, other_b = split_cores(place, factor, [(2, 1)])
    w0, w1, own_a, other_a = lax.optimization_barrier((w0, w1, own_a, other_a))
    other_a = shift(other_a, "core", 1, CORE)

    own_points = (train_points[:, 1:, 0] / lengthscales[:, None, None]).reshape(dims, -1)
    kernel = kernel_rows(own_points, scaled_new).reshape(panels - 1, block_rows, new_count)

    both = jnp.concatenate([part[0, block_rows:, : 2 * block_rows] for part in w0]).reshape(
        Y, dims // 2, 2, block_rows
    )
    line_points = both.transpose(2, 1, 0, 3).reshape(dims, Y, block_rows)
    line_points = (line_points / lengthscales[:, None, None]).reshape(dims, -1)
    residuals = kernel_rows(line_points, scaled_new).reshape(Y, block_rows, new_count)
    residuals = [residuals[e] for e in range(Y)]

    def reduce(keep, send):
        chip = keep + shift(send, "core", 1, CORE)
        return jnp.sum(lax.all_to_all(chip, "z", 0, 0), axis=0)

    def gather_z(rows):
        return lax.all_to_all(jnp.broadcast_to(rows[None], (Z,) + rows.shape), "z", 0, 0)

    def gather(line):
        return in_order(line, spread({e: line for e in range(1, Y)}))

    def residual_rows(panel, mine, theirs):
        own = mine + shift(theirs, "core", 1, CORE)
        arrived = [shift(own, "col", by, N_COL) for by in (2, 1, 3)]
        rest = kernel[panel - 1] - (own + arrived[0] + arrived[1] + arrived[2])
        return in_order(rest, spread({e: rest for e in range(1, Y)}))

    def solve(residuals, blocks, later, during_sum, during_gather):
        rows = reduce(*apply_inverse(place, residuals, blocks))
        far = spread(later, (2,))
        rows, far, later, during_sum = lax.optimization_barrier((rows, far, later, during_sum))
        line = gather_z(rows)
        near = spread(later, (1, 3))
        line, near, during_gather = lax.optimization_barrier((line, near, during_gather))
        return rows, line, in_order(later[0], {**far, **near}), during_sum, during_gather

    rows_0, line, w1, (w2, other_a), (own_b, other_b) = solve(
        residuals, w0, w1, (w2, other_a), (own_b, other_b)
    )
    blocks = (own_a, other_a)
    pieces = gather(line)
    residuals = residual_rows(1, *apply_factor(place, 0, blocks, pieces))
    early = apply_factor(place, 1, blocks, pieces)

    residuals, w2, early, other_b = lax.optimization_barrier((residuals, w2, early, other_b))
    other_b = shift(other_b, "core", 1, CORE)
    rows_1, line, w2, other_b, _ = solve(residuals, w1, w2, other_b, ())
    change = apply_factor(place, 0, (own_b, other_b), gather(line))
    residuals = residual_rows(2, early[0] + change[0], early[1] + change[1])

    rows_2 = reduce(*apply_inverse(place, residuals, w2))
    return jnp.stack([rows_0, rows_1, rows_2])[:, None, None]


def solution(mesh):
    split = Mesh(
        mesh.devices.reshape(Z, Y, CORE, mesh.devices.shape[1]), ("z", "y", "core", "col")
    )
    row = ("z", "y", "core")
    return jax.shard_map(
        on_device,
        mesh=split,
        in_specs=(
            P(None, None, row, None),
            P(),
            P(),
            P(None, row, None, None, "col", None),
            P(None, row, None, "col", None),
        ),
        out_specs=P(None, "col", row, None, None),
        check_vma=False,
    )
```

```python
import functools

import jax
import jax.numpy as jnp
from jax import lax
from jax.experimental import pallas as pl
from jax.experimental.pallas import tpu as pltpu
from jax.sharding import Mesh, PartitionSpec as P

Z, Y, CORE, N_COL = 8, 4, 2, 4
LANES = 128


def shift(value, axis, by, size):
    return lax.ppermute(value, axis, [(i, (i + by) % size) for i in range(size)])


def halves(value):
    high = value.astype(jnp.bfloat16)
    return high, (value - high.astype(jnp.float32)).astype(jnp.bfloat16)


def dot3(left, right, contract):
    left_high, left_low = left
    right_high, right_low = right
    dot = functools.partial(
        lax.dot_general,
        dimension_numbers=(contract, ((), ())),
        preferred_element_type=jnp.float32,
    )
    return dot(left_low, right_high) + dot(left_high, right_low) + dot(left_high, right_high)


def split_kernel(n_blocks, place, *refs):
    block_refs, extra_refs, outs, flat = refs[:n_blocks], refs[n_blocks : -Y - 1], refs[-Y - 1 : -1], refs[-1]
    y = place[1]
    rows, columns = flat.shape
    half = columns // (Z * Y)
    for at, block_ref in enumerate(block_refs):
        flat[...] = block_ref[...].reshape(rows, columns)
        left = lax.broadcasted_iota(jnp.int32, (rows, LANES), 1) < half
        for e in range(Y):
            to = lax.rem(y + e, Y)
            odd = lax.rem(to, 2) == 1
            for pair in range(Z // 2):
                tiles = []
                for z in (2 * pair, 2 * pair + 1):
                    start = pl.multiple_of((z * 2 + to // 2) * LANES, LANES)
                    tiles.append(flat[:, pl.ds(start, LANES)])
                first, second = tiles
                value = jnp.where(
                    left,
                    jnp.where(odd, pltpu.roll(first, half, axis=1), first),
                    jnp.where(odd, second, pltpu.roll(second, half, axis=1)),
                )
                outs[e][at, :rows, pair * LANES : (pair + 1) * LANES] = value
    for points_ref in extra_refs:
        more = points_ref.shape[0] // 2
        points = points_ref[...].reshape(2 * more, LANES)
        for out_ref in outs:
            out_ref[0, rows:, :] = jnp.zeros((more, out_ref.shape[2]), jnp.float32)
            out_ref[0, rows:, :LANES] = points[:more]
            out_ref[0, rows:, LANES : 2 * LANES] = points[more:]


def split_columns(place, blocks, extra=None):
    specs, arrays = [], []
    rows, columns = blocks[0][0].shape[2], blocks[0][0].shape[-1]
    for array, at in blocks:
        arrays.append(array)
        if array.ndim == 5:
            specs.append(
                pl.BlockSpec((None, None, rows, None, columns), lambda i, place, at=at: (at[0], 0, 0, 0, 0))
            )
        else:
            specs.append(
                pl.BlockSpec(
                    (None, None, rows, None, None, columns),
                    lambda i, place, at=at: (at[0], 0, 0, at[1], 0, 0),
                )
            )
    more = 0
    if extra is not None:
        arrays.append(extra)
        dims, _, _, width = extra.shape
        specs.append(pl.BlockSpec((dims, None, None, width), lambda i, place: (0, 0, 0, 0)))
        more = dims // 2
    out = jax.ShapeDtypeStruct((len(blocks), rows + more, columns // Y), jnp.float32)
    return pl.pallas_call(
        functools.partial(split_kernel, len(blocks)),
        out_shape=[out] * Y,
        grid_spec=pltpu.PrefetchScalarGridSpec(
            num_scalar_prefetch=1,
            grid=(1,),
            in_specs=specs,
            out_specs=[pl.BlockSpec(out.shape, lambda i, place: (0, 0, 0))] * Y,
            scratch_shapes=[pltpu.VMEM((rows, columns), jnp.float32)],
        ),
        cost_estimate=pl.CostEstimate(
            flops=len(blocks) * rows * columns,
            bytes_accessed=len(blocks) * rows * columns * 8,
            transcendentals=0,
        ),
        compiler_params=pltpu.CompilerParams(vmem_limit_bytes=54 << 20),
    )(place, *arrays)


def inverse_kernel(place, *refs):
    residuals, blocks = refs[:Y], refs[Y : 2 * Y]
    keep_ref, send_ref, high, low, product = refs[2 * Y :]
    core = place[2]
    rows = blocks[0].shape[0]
    parts = [halves(ref[...]) for ref in residuals]
    residual = tuple(jnp.concatenate([part[i] for part in parts]) for i in range(2))
    for e in range(Y):
        high[e * rows : (e + 1) * rows, :], low[e * rows : (e + 1) * rows, :] = halves(blocks[e][...])
    columns = high.shape[1]
    step = 256
    for start in range(0, columns, step):
        part = slice(start, start + step)
        product[part, :] = dot3((high[:, part], low[:, part]), residual, ((0,), (0,)))
    share = keep_ref.shape[1]
    for z in range(Z):
        for out_ref, owner in ((send_ref, 1 - core), (keep_ref, core)):
            start = pl.multiple_of((z * CORE + owner) * share, share)
            out_ref[z] = product[pl.ds(start, share), :]


def apply_inverse(place, residuals, blocks):
    rows, new = residuals[0].shape
    columns = blocks[0].shape[-1]
    out = jax.ShapeDtypeStruct((Z, columns // (Z * CORE), new), jnp.float32)
    return pl.pallas_call(
        inverse_kernel,
        out_shape=(out, out),
        grid_spec=pltpu.PrefetchScalarGridSpec(
            num_scalar_prefetch=1,
            grid=(1,),
            in_specs=[pl.BlockSpec((rows, new), lambda i, place: (0, 0))] * Y
            + [pl.BlockSpec((None, rows, columns), lambda i, place: (0, 0, 0))] * Y,
            out_specs=[pl.BlockSpec(out.shape, lambda i, place: (0, 0, 0))] * 2,
            scratch_shapes=[pltpu.VMEM((Y * rows, columns), jnp.bfloat16)] * 2
            + [pltpu.VMEM((columns, new), jnp.float32)],
        ),
        cost_estimate=pl.CostEstimate(
            flops=6 * Y * rows * columns * new, bytes_accessed=4 << 20, transcendentals=0
        ),
        compiler_params=pltpu.CompilerParams(vmem_limit_bytes=60 << 20),
    )(place, *residuals, *blocks)


def cores_kernel(n_blocks, place, *refs):
    block_refs, (own_ref, other_ref, flat) = refs[:n_blocks], refs[n_blocks:]
    core = place[2]
    rows, columns = flat.shape
    share = columns // (Z * Y * CORE)
    group = lax.broadcasted_iota(jnp.int32, (rows, LANES), 1) // share
    for at, block_ref in enumerate(block_refs):
        flat[...] = block_ref[...]
        for tile in range(columns // LANES // 2):
            first = flat[:, 2 * tile * LANES : (2 * tile + 1) * LANES]
            second = flat[:, (2 * tile + 1) * LANES : (2 * tile + 2) * LANES]

            def turned(value, groups):
                return pltpu.roll(value, groups % 4 * share, axis=1) if groups % 4 else value

            parts = [
                jnp.where(
                    group < 2,
                    jnp.where(group == 0, turned(first, -h), turned(first, -1 - h)),
                    jnp.where(group == 2, turned(second, 2 - h), turned(second, 1 - h)),
                )
                for h in range(CORE)
            ]
            where = slice(tile * LANES, (tile + 1) * LANES)
            own_ref[at, :, where] = jnp.where(core == 0, parts[0], parts[1])
            other_ref[at, :, where] = jnp.where(core == 0, parts[1], parts[0])


def split_cores(place, factor, blocks):
    rows, columns = factor.shape[2], factor.shape[5]
    out = jax.ShapeDtypeStruct((len(blocks), rows, columns // CORE), jnp.float32)
    return pl.pallas_call(
        functools.partial(cores_kernel, len(blocks)),
        out_shape=(out, out),
        grid_spec=pltpu.PrefetchScalarGridSpec(
            num_scalar_prefetch=1,
            grid=(1,),
            in_specs=[
                pl.BlockSpec(
                    (None, None, rows, None, None, columns),
                    lambda i, place, at=at: (at[0], 0, 0, at[1], 0, 0),
                )
                for at in blocks
            ],
            out_specs=[pl.BlockSpec(out.shape, lambda i, place: (0, 0, 0))] * 2,
            scratch_shapes=[pltpu.VMEM((rows, columns), jnp.float32)],
        ),
        cost_estimate=pl.CostEstimate(
            flops=8 * len(blocks) * rows * columns,
            bytes_accessed=8 * len(blocks) * rows * columns,
            transcendentals=0,
        ),
        compiler_params=pltpu.CompilerParams(vmem_limit_bytes=56 << 20),
    )(place, *[factor] * len(blocks))


def factor_kernel(place, own_ref, other_ref, *refs):
    pieces, (mine_ref, theirs_ref, high, low) = refs[:Y], refs[Y:]
    y = place[1]
    share = pieces[0].shape[1]

    def put(z, carry):
        for e in range(Y):
            row = z * Y + lax.rem(y + Y - e, Y)
            where = pl.ds(pl.multiple_of(row * share, share), share)
            high[where, :], low[where, :] = halves(pieces[e][z])
        return carry

    lax.fori_loop(0, Z, put, 0)
    for block_ref, out_ref in ((other_ref, theirs_ref), (own_ref, mine_ref)):
        out_ref[...] = dot3(halves(block_ref[...]), (high[...], low[...]), ((1,), (0,)))


def apply_factor(place, at, block, pieces):
    rows, columns = block[0].shape[1:]
    new = pieces[0].shape[-1]
    out = jax.ShapeDtypeStruct((rows, new), jnp.float32)
    return pl.pallas_call(
        factor_kernel,
        out_shape=(out, out),
        grid_spec=pltpu.PrefetchScalarGridSpec(
            num_scalar_prefetch=1,
            grid=(1,),
            in_specs=[pl.BlockSpec((None, rows, columns), lambda i, place: (at, 0, 0))] * 2
            + [pl.BlockSpec(pieces[0].shape, lambda i, place: (0, 0, 0))] * Y,
            out_specs=[pl.BlockSpec((rows, new), lambda i, place: (0, 0))] * 2,
            scratch_shapes=[pltpu.VMEM((columns, new), jnp.bfloat16)] * 2,
        ),
        cost_estimate=pl.CostEstimate(
            flops=12 * rows * columns * new, bytes_accessed=3 << 20, transcendentals=0
        ),
        compiler_params=pltpu.CompilerParams(vmem_limit_bytes=32 << 20),
    )(place, *block, *pieces)


def spread(arrays, steps=(2, 1, 3)):
    return {e: shift(arrays[e], "y", e, Y) for e in steps}


def in_order(own, arrived):
    return [own] + [arrived[e] for e in range(1, Y)]


def kernel_rows(scaled_train, scaled_new):
    inner_products = jnp.dot(scaled_train.T, scaled_new, precision=lax.Precision.HIGHEST)
    sqdist = (
        jnp.sum(scaled_train * scaled_train, axis=0)[:, None]
        + jnp.sum(scaled_new * scaled_new, axis=0)[None, :]
        - 2.0 * inner_products
    )
    return jnp.exp(-0.5 * sqdist)


def on_device(train_points, new_points, lengthscales, factor, diag_inverse):
    dims, panels, _, block_rows = train_points.shape
    new_count = new_points.shape[1]
    place = jnp.stack([lax.axis_index(axis) for axis in ("z", "y", "core")]).astype(jnp.int32)
    scaled_new = new_points / lengthscales[:, None]

    w0 = split_columns(place, [(diag_inverse, (0,))], train_points)
    w0 = in_order(w0[0], spread(w0))
    w1 = split_columns(place, [(diag_inverse, (1,))])
    w2 = split_columns(place, [(diag_inverse, (2,))])
    own_a, other_a = split_cores(place, factor, [(1, 0), (2, 0)])
    own_b, other_b = split_cores(place, factor, [(2, 1)])
    w0, w1, own_a, other_a = lax.optimization_barrier((w0, w1, own_a, other_a))
    other_a = shift(other_a, "core", 1, CORE)

    own_points = (train_points[:, 1:, 0] / lengthscales[:, None, None]).reshape(dims, -1)
    kernel = kernel_rows(own_points, scaled_new).reshape(panels - 1, block_rows, new_count)

    both = jnp.concatenate([part[0, block_rows:, : 2 * block_rows] for part in w0]).reshape(
        Y, dims // 2, 2, block_rows
    )
    line_points = both.transpose(2, 1, 0, 3).reshape(dims, Y, block_rows)
    line_points = (line_points / lengthscales[:, None, None]).reshape(dims, -1)
    residuals = kernel_rows(line_points, scaled_new).reshape(Y, block_rows, new_count)
    residuals = [residuals[e] for e in range(Y)]

    def reduce(keep, send):
        chip = keep + shift(send, "core", 1, CORE)
        return jnp.sum(lax.all_to_all(chip, "z", 0, 0), axis=0)

    def gather_z(rows):
        return lax.all_to_all(jnp.broadcast_to(rows[None], (Z,) + rows.shape), "z", 0, 0)

    def gather(line):
        return in_order(line, spread({e: line for e in range(1, Y)}))

    def residual_rows(panel, mine, theirs):
        own = mine + shift(theirs, "core", 1, CORE)
        arrived = [shift(own, "col", by, N_COL) for by in (2, 1, 3)]
        rest = kernel[panel - 1] - (own + arrived[0] + arrived[1] + arrived[2])
        return in_order(rest, spread({e: rest for e in range(1, Y)}))

    def solve(residuals, blocks, later, during_sum, during_gather):
        rows = reduce(*apply_inverse(place, residuals, blocks))
        far = spread(later, (2,))
        rows, far, later, during_sum = lax.optimization_barrier((rows, far, later, during_sum))
        line = gather_z(rows)
        near = spread(later, (1, 3))
        line, near, during_gather = lax.optimization_barrier((line, near, during_gather))
        return rows, line, in_order(later[0], {**far, **near}), during_sum, during_gather

    rows_0, line, w1, (w2, other_a), (own_b, other_b) = solve(
        residuals, w0, w1, (w2, other_a), (own_b, other_b)
    )
    blocks = (own_a, other_a)
    pieces = gather(line)
    residuals = residual_rows(1, *apply_factor(place, 0, blocks, pieces))
    early = apply_factor(place, 1, blocks, pieces)

    residuals, w2, early, other_b = lax.optimization_barrier((residuals, w2, early, other_b))
    other_b = shift(other_b, "core", 1, CORE)
    rows_1, line, w2, other_b, _ = solve(residuals, w1, w2, other_b, ())
    change = apply_factor(place, 0, (own_b, other_b), gather(line))
    residuals = residual_rows(2, early[0] + change[0], early[1] + change[1])

    rows_2 = reduce(*apply_inverse(place, residuals, w2))
    return jnp.stack([rows_0, rows_1, rows_2])[:, None, None]


def solution(mesh):
    split = Mesh(
        mesh.devices.reshape(Z, Y, CORE, mesh.devices.shape[1]), ("z", "y", "core", "col")
    )
    row = ("z", "y", "core")
    return jax.shard_map(
        on_device,
        mesh=split,
        in_specs=(
            P(None, None, row, None),
            P(),
            P(),
            P(None, row, None, None, "col", None),
            P(None, row, None, "col", None),
        ),
        out_specs=P(None, "col", row, None, None),
        check_vma=False,
    )
```

```python
import functools

import jax
import jax.numpy as jnp
from jax import lax
from jax.experimental import pallas as pl
from jax.experimental.pallas import tpu as pltpu
from jax.sharding import Mesh, PartitionSpec as P

Z, Y, CORE, N_COL = 8, 4, 2, 4
LANES = 128


def shift(value, axis, by, size):
    return lax.ppermute(value, axis, [(i, (i + by) % size) for i in range(size)])


def halves(value):
    high = value.astype(jnp.bfloat16)
    return high, (value - high.astype(jnp.float32)).astype(jnp.bfloat16)


def dot3(left, right, contract):
    left_high, left_low = left
    right_high, right_low = right
    dot = functools.partial(
        lax.dot_general,
        dimension_numbers=(contract, ((), ())),
        preferred_element_type=jnp.float32,
    )
    return dot(left_low, right_high) + dot(left_high, right_low) + dot(left_high, right_high)


def split_kernel(n_blocks, place, *refs):
    block_refs, extra_refs, outs, flat = refs[:n_blocks], refs[n_blocks : -Y - 1], refs[-Y - 1 : -1], refs[-1]
    y = place[1]
    rows, columns = flat.shape
    half = columns // (Z * Y)
    for at, block_ref in enumerate(block_refs):
        flat[...] = block_ref[...].reshape(rows, columns)
        left = lax.broadcasted_iota(jnp.int32, (rows, LANES), 1) < half
        for e in range(Y):
            to = lax.rem(y + e, Y)
            odd = lax.rem(to, 2) == 1
            for pair in range(Z // 2):
                tiles = []
                for z in (2 * pair, 2 * pair + 1):
                    start = pl.multiple_of((z * 2 + to // 2) * LANES, LANES)
                    tiles.append(flat[:, pl.ds(start, LANES)])
                first, second = tiles
                value = jnp.where(
                    left,
                    jnp.where(odd, pltpu.roll(first, half, axis=1), first),
                    jnp.where(odd, second, pltpu.roll(second, half, axis=1)),
                )
                outs[e][at, :rows, pair * LANES : (pair + 1) * LANES] = value
    for points_ref in extra_refs:
        more = points_ref.shape[0] // 2
        points = points_ref[...].reshape(2 * more, LANES)
        for out_ref in outs:
            out_ref[0, rows:, :] = jnp.zeros((more, out_ref.shape[2]), jnp.float32)
            out_ref[0, rows:, :LANES] = points[:more]
            out_ref[0, rows:, LANES : 2 * LANES] = points[more:]


def split_columns(place, blocks, extra=None):
    specs, arrays = [], []
    rows, columns = blocks[0][0].shape[2], blocks[0][0].shape[-1]
    for array, at in blocks:
        arrays.append(array)
        if array.ndim == 5:
            specs.append(
                pl.BlockSpec((None, None, rows, None, columns), lambda i, place, at=at: (at[0], 0, 0, 0, 0))
            )
        else:
            specs.append(
                pl.BlockSpec(
                    (None, None, rows, None, None, columns),
                    lambda i, place, at=at: (at[0], 0, 0, at[1], 0, 0),
                )
            )
    more = 0
    if extra is not None:
        arrays.append(extra)
        dims, _, _, width = extra.shape
        specs.append(pl.BlockSpec((dims, None, None, width), lambda i, place: (0, 0, 0, 0)))
        more = dims // 2
    out = jax.ShapeDtypeStruct((len(blocks), rows + more, columns // Y), jnp.float32)
    return pl.pallas_call(
        functools.partial(split_kernel, len(blocks)),
        out_shape=[out] * Y,
        grid_spec=pltpu.PrefetchScalarGridSpec(
            num_scalar_prefetch=1,
            grid=(1,),
            in_specs=specs,
            out_specs=[pl.BlockSpec(out.shape, lambda i, place: (0, 0, 0))] * Y,
            scratch_shapes=[pltpu.VMEM((rows, columns), jnp.float32)],
        ),
        cost_estimate=pl.CostEstimate(
            flops=len(blocks) * rows * columns,
            bytes_accessed=len(blocks) * rows * columns * 8,
            transcendentals=0,
        ),
        compiler_params=pltpu.CompilerParams(vmem_limit_bytes=54 << 20),
    )(place, *arrays)


def inverse_kernel(place, *refs):
    residuals, blocks = refs[:Y], refs[Y : 2 * Y]
    keep_ref, send_ref, high, low, product = refs[2 * Y :]
    core = place[2]
    rows = blocks[0].shape[0]
    parts = [halves(ref[...]) for ref in residuals]
    residual = tuple(jnp.concatenate([part[i] for part in parts]) for i in range(2))
    for e in range(Y):
        high[e * rows : (e + 1) * rows, :], low[e * rows : (e + 1) * rows, :] = halves(blocks[e][...])
    columns = high.shape[1]
    step = 256
    for start in range(0, columns, step):
        part = slice(start, start + step)
        product[part, :] = dot3((high[:, part], low[:, part]), residual, ((0,), (0,)))
    share = keep_ref.shape[1]
    for z in range(Z):
        for out_ref, owner in ((send_ref, 1 - core), (keep_ref, core)):
            start = pl.multiple_of((z * CORE + owner) * share, share)
            out_ref[z] = product[pl.ds(start, share), :]


def apply_inverse(place, residuals, blocks):
    rows, new = residuals[0].shape
    columns = blocks[0].shape[-1]
    out = jax.ShapeDtypeStruct((Z, columns // (Z * CORE), new), jnp.float32)
    return pl.pallas_call(
        inverse_kernel,
        out_shape=(out, out),
        grid_spec=pltpu.PrefetchScalarGridSpec(
            num_scalar_prefetch=1,
            grid=(1,),
            in_specs=[pl.BlockSpec((rows, new), lambda i, place: (0, 0))] * Y
            + [pl.BlockSpec((None, rows, columns), lambda i, place: (0, 0, 0))] * Y,
            out_specs=[pl.BlockSpec(out.shape, lambda i, place: (0, 0, 0))] * 2,
            scratch_shapes=[pltpu.VMEM((Y * rows, columns), jnp.bfloat16)] * 2
            + [pltpu.VMEM((columns, new), jnp.float32)],
        ),
        cost_estimate=pl.CostEstimate(
            flops=6 * Y * rows * columns * new, bytes_accessed=4 << 20, transcendentals=0
        ),
        compiler_params=pltpu.CompilerParams(vmem_limit_bytes=32 << 20),
    )(place, *residuals, *blocks)


def halve_kernel(block_ref, high_ref, low_ref, flat):
    flat[...] = block_ref[...]
    step = 16

    def part(i, carry):
        where = pl.ds(pl.multiple_of(i * step, step), step)
        high_ref[where, :], low_ref[where, :] = halves(flat[where, :])
        return carry

    lax.fori_loop(0, flat.shape[0] // step, part, 0)


def halve_block(factor, row, column):
    rows, columns = factor.shape[2], factor.shape[5]
    out = jax.ShapeDtypeStruct((rows, columns), jnp.bfloat16)
    return pl.pallas_call(
        halve_kernel,
        out_shape=(out, out),
        grid=(1,),
        in_specs=[
            pl.BlockSpec(
                (None, None, rows, None, None, columns), lambda i: (row, 0, 0, column, 0, 0)
            )
        ],
        out_specs=[pl.BlockSpec(out.shape, lambda i: (0, 0))] * 2,
        scratch_shapes=[pltpu.VMEM(out.shape, jnp.float32)],
        cost_estimate=pl.CostEstimate(
            flops=4 * rows * columns, bytes_accessed=8 * rows * columns, transcendentals=0
        ),
        compiler_params=pltpu.CompilerParams(vmem_limit_bytes=56 << 20),
    )(factor)


def factor_kernel(place, block_high, block_low, *refs):
    pieces, rest, (out_ref, high, low) = refs[: Y + 2], refs[Y + 2], refs[Y + 3 :]
    y, core = place[1], place[2]
    share = pieces[0].shape[1]

    def put(z, carry):
        for at, owner in enumerate((core, 1 - core)):
            for e in range(Y):
                row = (z * Y + lax.rem(y + Y - e, Y)) * CORE + owner
                where = pl.ds(pl.multiple_of(row * share, share), share)
                piece = rest[e - 2, z] if at and e > 1 else pieces[at * Y + e][z]
                high[where, :], low[where, :] = halves(piece)
        return carry

    lax.fori_loop(0, Z, put, 0)
    out_ref[...] = dot3(
        (block_high[...], block_low[...]), (high[...], low[...]), ((1,), (0,))
    )


def apply_factor(place, block, pieces):
    rows, columns = block[0].shape
    new = pieces[0].shape[-1]
    return pl.pallas_call(
        factor_kernel,
        out_shape=jax.ShapeDtypeStruct((rows, new), jnp.float32),
        grid_spec=pltpu.PrefetchScalarGridSpec(
            num_scalar_prefetch=1,
            grid=(1,),
            in_specs=[pl.BlockSpec((rows, columns), lambda i, place: (0, 0))] * 2
            + [pl.BlockSpec(pieces[0].shape, lambda i, place: (0, 0, 0))] * (Y + 2)
            + [pl.BlockSpec(pieces[-1].shape, lambda i, place: (0, 0, 0, 0))],
            out_specs=pl.BlockSpec((rows, new), lambda i, place: (0, 0)),
            scratch_shapes=[pltpu.VMEM((columns, new), jnp.bfloat16)] * 2,
        ),
        cost_estimate=pl.CostEstimate(
            flops=6 * rows * columns * new, bytes_accessed=3 << 20, transcendentals=0
        ),
        compiler_params=pltpu.CompilerParams(vmem_limit_bytes=32 << 20),
    )(place, *block, *pieces)


def spread(arrays, steps=(2, 1, 3)):
    return {e: shift(arrays[e], "y", e, Y) for e in steps}


def in_order(own, arrived):
    return [own] + [arrived[e] for e in range(1, Y)]


def kernel_rows(scaled_train, scaled_new):
    inner_products = jnp.dot(scaled_train.T, scaled_new, precision=lax.Precision.HIGHEST)
    sqdist = (
        jnp.sum(scaled_train * scaled_train, axis=0)[:, None]
        + jnp.sum(scaled_new * scaled_new, axis=0)[None, :]
        - 2.0 * inner_products
    )
    return jnp.exp(-0.5 * sqdist)


def on_device(train_points, new_points, lengthscales, factor, diag_inverse):
    dims, panels, _, block_rows = train_points.shape
    new_count = new_points.shape[1]
    place = jnp.stack([lax.axis_index(axis) for axis in ("z", "y", "core")]).astype(jnp.int32)
    scaled_new = new_points / lengthscales[:, None]

    w0 = split_columns(place, [(diag_inverse, (0,))], train_points)
    w0 = in_order(w0[0], spread(w0))
    w1 = split_columns(place, [(diag_inverse, (1,))])
    w2 = split_columns(place, [(diag_inverse, (2,))])
    l10, l20, l21 = (halve_block(factor, *at) for at in ((1, 0), (2, 0), (2, 1)))
    w0, w1, l10, l20 = lax.optimization_barrier((w0, w1, l10, l20))

    own_points = (train_points[:, 1:, 0] / lengthscales[:, None, None]).reshape(dims, -1)
    kernel = kernel_rows(own_points, scaled_new).reshape(panels - 1, block_rows, new_count)

    both = jnp.concatenate([part[0, block_rows:, : 2 * block_rows] for part in w0]).reshape(
        Y, dims // 2, 2, block_rows
    )
    line_points = both.transpose(2, 1, 0, 3).reshape(dims, Y, block_rows)
    line_points = (line_points / lengthscales[:, None, None]).reshape(dims, -1)
    residuals = kernel_rows(line_points, scaled_new).reshape(Y, block_rows, new_count)
    residuals = [residuals[e] for e in range(Y)]

    def reduce(keep, send):
        chip = keep + shift(send, "core", 1, CORE)
        return jnp.sum(lax.all_to_all(chip, "z", 0, 0), axis=0)

    def gather_z(rows):
        return lax.all_to_all(jnp.broadcast_to(rows[None], (Z,) + rows.shape), "z", 0, 0)

    def gather(line):
        mine = in_order(line, spread({e: line for e in range(1, Y)}))
        rest = shift(jnp.stack(mine[2:]), "core", 1, CORE)
        return mine + [shift(piece, "core", 1, CORE) for piece in mine[:2]] + [rest]

    def residual_rows(panel, own):
        arrived = [shift(own, "col", by, N_COL) for by in (2, 1, 3)]
        rest = kernel[panel - 1] - (own + arrived[0] + arrived[1] + arrived[2])
        return in_order(rest, spread({e: rest for e in range(1, Y)}))

    def solve(residuals, blocks, later, during_sum, during_gather):
        rows = reduce(*apply_inverse(place, residuals, blocks))
        far = spread(later, (2,))
        rows, far, later, during_sum = lax.optimization_barrier((rows, far, later, during_sum))
        line = gather_z(rows)
        near = spread(later, (1, 3))
        line, near, during_gather = lax.optimization_barrier((line, near, during_gather))
        return rows, line, in_order(later[0], {**far, **near}), during_sum, during_gather

    rows_0, line, w1, w2, l21 = solve(residuals, w0, w1, w2, l21)
    pieces = gather(line)
    residuals = residual_rows(1, apply_factor(place, l10, pieces))
    early = apply_factor(place, l20, pieces)

    residuals, w2, early = lax.optimization_barrier((residuals, w2, early))
    rows_1, line, w2, _, _ = solve(residuals, w1, w2, (), ())
    pieces = gather(line)
    residuals = residual_rows(2, early + apply_factor(place, l21, pieces))

    rows_2 = reduce(*apply_inverse(place, residuals, w2))
    return jnp.stack([rows_0, rows_1, rows_2])[:, None, None]


def solution(mesh):
    split = Mesh(
        mesh.devices.reshape(Z, Y, CORE, mesh.devices.shape[1]), ("z", "y", "core", "col")
    )
    row = ("z", "y", "core")
    return jax.shard_map(
        on_device,
        mesh=split,
        in_specs=(
            P(None, None, row, None),
            P(),
            P(),
            P(None, row, None, None, "col", None),
            P(None, row, None, "col", None),
        ),
        out_specs=P(None, "col", row, None, None),
        check_vma=False,
    )
```
